32 devices in a mesh: cells: 2 (over y), genes: 16 (over z, x, core).
Axes of the slice: x: 2, y: 2, z: 4, core: 2. Of those that a mesh axis runs over, the one named last changes fastest.
Arguments:
- expression: float32 [320, 32768], P('cells', 'genes'), may hold values from -6 to 6
- omega_diag: float32 [128, 256, 256], P('genes'), may hold values from -0.25 to 2, as said below
- omega_offd: float32 [128, 6, 256, 256], P('genes'), may hold values from -0.3 to 0.3
- omega_src: int32 [128, 6], replicated, may hold values from 0 to 15, all different within a row; in each aligned block of 8 rows (0 to 7, 8 to 15, ...) at most 3 rows name the same one
- omega_off: int32 [128, 6], replicated, may hold values from 0 to 6
Outputs:
- new_diag: float32 [128, 256, 256], P(('genes', 'cells'))
- new_offd: float32 [128, 6, 256, 256], P(('genes', 'cells'))
The draws below stay inside these ranges and needn't reach their ends.
Inputs may be any that keep to these rules, and one draw needn't show every extreme that they name: `omega_src`: the 6 values of one row are distinct. Among the 8 rows of one index of genes (rows i * 8 to (i+1) * 8 - 1) no value appears more than 3 times, and in every draw some such group of rows names some value exactly 3 times. `omega_diag`: diagonal entries lie in 0.5 to 2; all other entries lie in -0.25 to 0.25.
All inputs are finite; a program needn't handle non-finite values.
Results may differ from the reference program's by a relative error of at most 0.000075.
Values sent between devices are 32-bit elements; how exact they have to be, the bound alone decides.
A program may use at most 192 MiB of HBM per device.

```python
import math
import jax
import jax.numpy as jnp
import numpy as np
from jax import lax

BS = 256
K = 6
BLOCKS_DEV = 8
NBLK = 128
GENES = 32768
CELLS = 320
MOST = 3
N_GENES = 16


def draw_omega_diag(key, part):
    first, second = jax.random.split(jax.random.fold_in(key, 17))
    spread = jnp.clip(0.05 * jax.random.normal(first, (NBLK, BS, BS), jnp.float32), -0.25, 0.25)
    entries = jax.random.uniform(second, (NBLK, BS), jnp.float32, 0.5, 2.0)
    eye = jnp.eye(BS, dtype=jnp.float32)
    return spread * (1.0 - eye) + entries[:, :, None] * eye


def touch_ends(values, own_key, least, largest):
    longest = values.shape.index(max(values.shape))
    spots = []
    for shift in (0, 1):
        where = [jax.random.randint(jax.random.fold_in(own_key, axis), (), 0, length) for axis, length in enumerate(values.shape)]
        where[longest] = (where[longest] + shift) % values.shape[longest]
        spots.append(tuple(where))
    return values.at[spots[0]].set(least).at[spots[1]].set(largest)


def levels(rng, extent, cuts, smallest, high):
    gain, own = 1.0, jax.random.fold_in(rng, 6)
    for position, parts in cuts:
        heights = jnp.exp(jax.random.uniform(jax.random.fold_in(own, position), (parts,), jnp.float32, smallest / len(cuts), high / len(cuts)))
        gain = gain * jnp.repeat(heights, extent[position] // parts).reshape([-1 if axis == position else 1 for axis in range(len(extent))])
    return gain


def shared_out(rng, own, number, rows, number_of, top, reach, slope):
    sequence = jax.random.permutation(rng, number_of)
    crowded, usual = load_shares(number_of, rows * top, reach, slope, True), load_shares(number_of, rows * top, reach, slope, False)
    places = jnp.arange(number_of)

    def named(tallies, rotation):
        used = int((tallies > 0).sum())
        fixed = max(1, used // 4)
        shifted = fixed + (places - fixed + rotation * (used - fixed)) % max(1, number_of - fixed)
        return jnp.zeros((number_of,), jnp.int32).at[sequence[jnp.where(places < fixed, places, shifted)]].set(jnp.asarray(tallies, jnp.int32))

    tallies = jnp.where(number % 4 == 0, named(crowded, number // 4), named(usual, number - number // 4 - 1))
    mixed = jax.random.permutation(jax.random.fold_in(own, 3), number_of)
    donor, sink = mixed[0:number_of // 2 * 2:2], mixed[1:number_of // 2 * 2:2]
    slack = jnp.minimum(tallies[donor] - 1, reach - tallies[sink]) // 2
    slack = jnp.where((donor == sequence[0]) | (sink == sequence[0]) | (tallies[sink] == 0), 0, jnp.maximum(slack, 0))
    shifted = jax.random.randint(jax.random.fold_in(own, 4), (number_of // 2,), 0, 1 << 20) % (slack + 1)
    tallies = tallies.at[donor].add(-shifted).at[sink].add(shifted)
    members = jnp.searchsorted(jnp.cumsum(tallies), jnp.arange(rows * top), side="right").astype(jnp.int32)
    table = members.reshape(top, rows).T
    table = table[jax.random.permutation(jax.random.fold_in(own, 1), rows)]
    rotation = jax.random.randint(jax.random.fold_in(own, 2), (rows, 1), 0, top)
    return jnp.take_along_axis(table, (jnp.arange(top)[None, :] + rotation) % top, axis=1)


def load_shares(count, total, most, skew, full):
    loads = [(1 << 20) // math.isqrt(grade ** skew) + 1 for grade in range(1, count + 1)]
    largest = most if full else min(most, max(-(-total // count), total * loads[0] // sum(loads)))
    least = 1 if total - largest >= count - 1 else 0
    counts, spare = [largest] + [least] * (count - 1), total - largest - least * (count - 1)
    while spare > 0:
        free = [i for i in range(1, count) if counts[i] < largest] or [i for i in range(1, count) if counts[i] < most]
        whole, remaining = sum([loads[i] for i in free]), spare
        for i in free:
            more = min(most - counts[i], max(1, remaining * loads[i] // whole), spare)
            counts[i] = counts[i] + more
            spare = spare - more
    return np.array(counts)


def gaussian(stream_key, dims, width, most, cuts=(), kind=jnp.bfloat16):
    level = levels(stream_key, dims, cuts, -0.22, 0.18) if cuts else 1.0
    values = jax.random.normal(stream_key, dims, jnp.float32) * width * level
    return jnp.minimum(jnp.maximum(values, -most), most).astype(kind)


def setup_inputs(seed: int = 0) -> dict:
    arg_keys = jax.random.split(jax.random.key(seed), 6)
    expression = gaussian(arg_keys[0], (CELLS, GENES), 1.0, 6.0, ((0, 2), (1, 16)), jnp.float32)
    omega_diag = draw_omega_diag(jax.random.fold_in(arg_keys[5], 71), 0)
    omega_offd = gaussian(arg_keys[2], (NBLK, K, BS, BS), 0.05, 0.3, ((0, 16),), jnp.float32)
    omega_src_keys = jax.random.split(jax.random.fold_in(arg_keys[3], 1), NBLK // BLOCKS_DEV)
    omega_src_turns = jax.random.permutation(jax.random.fold_in(arg_keys[3], 3), NBLK // BLOCKS_DEV)
    omega_src = jax.vmap(lambda own, number: shared_out(jax.random.fold_in(arg_keys[3], 2), own, number, BLOCKS_DEV, N_GENES, K, MOST, 2))(omega_src_keys, omega_src_turns).reshape((NBLK, K))
    omega_off = touch_ends(jax.random.randint(arg_keys[4], (NBLK, K), 0, BLOCKS_DEV - 1), jax.random.fold_in(arg_keys[4], 1), 0, (BLOCKS_DEV - 1) - 1).astype(jnp.int32)
    return {"expression": expression, "omega_diag": omega_diag, "omega_offd": omega_offd, "omega_src": omega_src, "omega_off": omega_off}


def stored_rows(omega_src, omega_off, per_dev):
    cols = lax.broadcasted_iota(jnp.int32, omega_src.shape, 0)
    bump = jnp.logical_and(omega_src == cols // per_dev, omega_off >= cols % per_dev).astype(jnp.int32)
    return omega_src * per_dev + omega_off + bump


def shrink(values, limit):
    return values - jnp.clip(values, -limit, limit)


def reference(expression, omega_diag, omega_offd, omega_src, omega_off):
    highest = lax.Precision.HIGHEST
    cell_count = expression.shape[0]
    rows = stored_rows(omega_src, omega_off, BLOCKS_DEV)
    blocks = expression.reshape(cell_count, NBLK, BS)

    def column(j):
        own = lax.dynamic_index_in_dim(blocks, j, 1, keepdims=False)
        far = jnp.take(blocks, rows[j], axis=1)
        first = jnp.dot(own, omega_diag[j], precision=highest, preferred_element_type=omega_diag.dtype)
        return first + jnp.einsum('ckb,kbe->ce', far, omega_offd[j], precision=highest)

    outputs = lax.map(column, jnp.arange(NBLK, dtype=jnp.int32))

    def gradient(j):
        own_x = lax.dynamic_index_in_dim(blocks, j, 1, keepdims=False)
        own_y = outputs[j]
        far_x = jnp.take(blocks, rows[j], axis=1)
        far_y = jnp.take(outputs, rows[j], axis=0)
        diag_part = jnp.einsum('cb,ce->be', own_x, own_y, precision=highest)
        diag_part = diag_part + diag_part.T
        off_part = jnp.einsum('ckb,ce->kbe', far_x, own_y, precision=highest)
        off_part = off_part + jnp.einsum('kcb,ce->kbe', far_y, own_x, precision=highest)
        return diag_part, off_part

    diag_sum, off_sum = lax.map(gradient, jnp.arange(NBLK, dtype=jnp.int32))
    step_size = 0.5
    limit = step_size * 0.04
    scale = 1.0 / (2.0 * cell_count)
    eye = (lax.broadcasted_iota(jnp.int32, (BS, BS), 0) == lax.broadcasted_iota(jnp.int32, (BS, BS), 1)).astype(omega_diag.dtype)
    entries = jnp.sum(omega_diag * eye, axis=2)
    grad_diag = diag_sum * scale - eye * (1.0 / entries)[:, :, None]
    moved = omega_diag - step_size * grad_diag
    new_diag = eye * moved + (1.0 - eye) * shrink(moved, limit)
    new_offd = shrink(omega_offd - step_size * (off_sum * scale), limit)
    return new_diag, new_offd
```

```python
import jax
import jax.numpy as jnp
from jax import lax
from jax.sharding import PartitionSpec as P


def stored_rows(omega_src, omega_off, per_dev):
    cols = lax.broadcasted_iota(jnp.int32, omega_src.shape, 0)
    bump = jnp.logical_and(omega_src == cols // per_dev, omega_off >= cols % per_dev).astype(
        jnp.int32
    )
    return omega_src * per_dev + omega_off + bump


def shrink(values, limit):
    return values - jnp.clip(values, -limit, limit)


def exchange(shard, table):
    whole = lax.all_gather(shard, "genes", axis=0, tiled=True)
    picked = jnp.take(whole, table, axis=0)
    return lax.all_to_all(picked, "cells", split_axis=0, concat_axis=1, tiled=True)


def per_device(expression, omega_diag, omega_offd, omega_src, omega_off):
    high = lax.Precision.HIGH
    here = lax.axis_index("genes")
    where = lax.axis_index("cells")
    cells = lax.axis_size("cells")
    per_dev, width = omega_diag.shape[:2]
    fan = omega_src.shape[1]
    cell_rows = expression.shape[0]
    share = per_dev // cells
    all_rows = cells * cell_rows
    rows = stored_rows(omega_src, omega_off, per_dev)
    table = lax.dynamic_slice_in_dim(rows, here * per_dev, per_dev, 0).reshape(-1)
    mine_diag = lax.dynamic_slice_in_dim(omega_diag, where * share, share, 0)
    mine_off = lax.dynamic_slice_in_dim(omega_offd, where * share, share, 0)

    shard_x = jnp.swapaxes(expression.reshape(cell_rows, per_dev, width), 0, 1)
    own_x = lax.all_to_all(shard_x, "cells", split_axis=0, concat_axis=1, tiled=True)
    far_x = exchange(shard_x, table).reshape(share, fan, all_rows, width)
    own_y = jnp.einsum("jcb,jbe->jce", own_x, mine_diag, precision=high)
    own_y = own_y + jnp.einsum("jkcb,jkbe->jce", far_x, mine_off, precision=high)
    shard_y = lax.all_to_all(own_y, "cells", split_axis=1, concat_axis=0, tiled=True)
    far_y = exchange(shard_y, table).reshape(share, fan, all_rows, width)
    diag_sum = jnp.einsum("jcb,jce->jbe", own_x, own_y, precision=high)
    diag_sum = diag_sum + jnp.swapaxes(diag_sum, 1, 2)
    off_sum = jnp.einsum("jkcb,jce->jkbe", far_x, own_y, precision=high)
    off_sum = off_sum + jnp.einsum("jkcb,jce->jkbe", far_y, own_x, precision=high)

    step_size = 0.5
    limit = step_size * 0.04
    scale = 1.0 / (2.0 * all_rows)
    eye = (
        lax.broadcasted_iota(jnp.int32, (width, width), 0)
        == lax.broadcasted_iota(jnp.int32, (width, width), 1)
    ).astype(jnp.float32)
    entries = jnp.sum(mine_diag * eye, axis=2)
    grad_diag = diag_sum * scale - eye * (1.0 / entries)[:, :, None]
    moved = mine_diag - step_size * grad_diag
    new_diag = eye * moved + (1.0 - eye) * shrink(moved, limit)
    new_offd = shrink(mine_off - step_size * (off_sum * scale), limit)
    return (new_diag, new_offd)


def solution(mesh):
    return jax.shard_map(
        per_device,
        mesh=mesh,
        in_specs=(
            P("cells", "genes"),
            P("genes", None, None),
            P("genes", None, None, None),
            P(),
            P(),
        ),
        out_specs=(P(("genes", "cells"), None, None), P(("genes", "cells"), None, None, None)),
        check_vma=False,
    )
```

```python
import functools

import jax
import jax.numpy as jnp
from jax import lax
from jax.experimental import pallas as pl
from jax.experimental.pallas import tpu as pltpu
from jax.sharding import PartitionSpec as P

MESH = pl.DeviceIdType.MESH


def stored_rows(omega_src, omega_off, per_dev):
    cols = lax.broadcasted_iota(jnp.int32, omega_src.shape, 0)
    bump = jnp.logical_and(omega_src == cols // per_dev, omega_off >= cols % per_dev).astype(
        jnp.int32
    )
    return omega_src * per_dev + omega_off + bump


def shrink(values, limit):
    return values - jnp.clip(values, -limit, limit)


def exchange_kernel(chunks, table_ref, shard_ref, far_ref, *scratch):
    held, picked = scratch[:chunks], scratch[chunks : 2 * chunks]
    z_send, x_send, k_send, got, c_send, c_got, own_sem = scratch[2 * chunks :]
    groups, cells = lax.axis_size("genes"), lax.axis_size("cells")
    me, part = lax.axis_index("genes"), lax.axis_index("cells")
    line = groups // 4
    per_dev, cell_rows, _ = shard_ref.shape
    size = cell_rows // chunks
    entries = far_ref.shape[0]
    z, lane = me // 4, me % 4
    other_x = lane + 2 - 4 * (lane // 2)
    other_k = me + 1 - 2 * (me % 2)
    x_peer = z * 4 + other_x

    def to_gene(gene):
        return (part, gene)

    def to_cell(step):
        return ((part + step) % cells, me)

    barrier = pltpu.get_barrier_semaphore()
    ahead, behind = (z + 1) % line * 4 + lane, (z + line - 1) % line * 4 + lane
    for gene in (ahead, behind, x_peer, other_k):
        pl.semaphore_signal(barrier, inc=1, device_id=to_gene(gene), device_id_type=MESH)
    for step in range(1, cells):
        pl.semaphore_signal(barrier, inc=1, device_id=to_cell(step), device_id_type=MESH)
    pl.semaphore_wait(barrier, 4 + cells - 1)

    def seat(chunk, gene):
        return held[chunk].at[pl.ds(gene * per_dev, per_dev)]

    def own(chunk):
        return shard_ref.at[:, pl.ds(chunk * size, size), :]

    def copy(chunk, gene, send_sem, target, first=False):
        return pltpu.make_async_remote_copy(
            src_ref=own(chunk) if first else seat(chunk, gene),
            dst_ref=seat(chunk, gene),
            send_sem=send_sem,
            recv_sem=got.at[chunk, gene],
            device_id=to_gene(target),
            device_id_type=MESH,
        )

    def arrive(chunk, gene):
        copy(chunk, gene, k_send.at[chunk, gene], other_k).wait_recv()

    def keep(chunk):
        return pltpu.make_async_copy(own(chunk), seat(chunk, me), own_sem.at[chunk])

    def up(chunk, gene, first=False):
        return copy(chunk, gene, z_send.at[chunk, gene, 0], me + 4, first)

    def down(chunk, gene, first=False):
        return copy(chunk, gene, z_send.at[chunk, gene, 1], me - 4, first)

    def across(chunk, gene, first=False):
        return copy(chunk, gene, x_send.at[chunk, gene], x_peer, first)

    def beside(chunk, gene, first=False):
        return copy(chunk, gene, k_send.at[chunk, gene], other_k, first)

    def start_own(chunk):
        pl.when(z < line - 1)(lambda: up(chunk, me, True).start())
        pl.when(z > 0)(lambda: down(chunk, me, True).start())
        across(chunk, me, True).start()
        beside(chunk, me, True).start()
        keep(chunk).start()

    def relay(chunk, distance):
        @pl.when(z - distance >= 0)
        def _():
            gene = me - 4 * distance
            arrive(chunk, gene)
            pl.when(z < line - 1)(lambda: up(chunk, gene).start())
            across(chunk, gene).start()
            beside(chunk, gene).start()

        @pl.when(z + distance < line)
        def _():
            gene = me + 4 * distance
            arrive(chunk, gene)
            pl.when(z > 0)(lambda: down(chunk, gene).start())
            across(chunk, gene).start()
            beside(chunk, gene).start()

    def cross_over(chunk):
        for at in range(line):
            gene = at * 4 + other_x
            arrive(chunk, gene)
            beside(chunk, gene).start()

    def row_span(chunk, cell):
        return pl.ds(pl.multiple_of(cell * cell_rows + chunk * size, 8), size)

    def hand(chunk, step):
        return pltpu.make_async_remote_copy(
            src_ref=picked[chunk].at[step - 1],
            dst_ref=far_ref.at[:, row_span(chunk, part), :],
            send_sem=c_send.at[chunk, step],
            recv_sem=c_got.at[chunk, step],
            device_id=to_cell(step),
            device_id_type=MESH,
        )

    def pick(chunk):
        keep(chunk).wait()
        for at in range(line):
            for side in range(2):
                arrive(chunk, at * 4 + side * 2 + other_k % 2)
        for step in list(range(1, cells)) + [0]:
            base = (part + step) % cells * entries

            def body(entry, carry):
                block = held[chunk][table_ref[base + entry]]
                if step == 0:
                    far_ref[entry, row_span(chunk, part), :] = block
                else:
                    picked[chunk][step - 1, entry] = block
                return carry

            lax.fori_loop(0, entries, body, 0)
            if step:
                hand(chunk, step).start()

    for t in range(chunks + line + 1):
        if t < chunks:
            start_own(t)
        for distance in range(1, line):
            if 0 <= t - distance < chunks:
                relay(t - distance, distance)
        if 0 <= t - line < chunks:
            cross_over(t - line)
        if 0 <= t - line - 1 < chunks:
            pick(t - line - 1)

    for chunk in range(chunks):
        for step in range(1, cells):
            hand(chunk, step).wait_recv()
            hand(chunk, step).wait_send()
        pl.when(z < line - 1)(lambda: up(chunk, me, True).wait_send())
        pl.when(z > 0)(lambda: down(chunk, me, True).wait_send())
        across(chunk, me, True).wait_send()
        beside(chunk, me, True).wait_send()
        for distance in range(1, line):

            @pl.when(z - distance >= 0)
            def _():
                gene = me - 4 * distance
                pl.when(z < line - 1)(lambda: up(chunk, gene).wait_send())
                across(chunk, gene).wait_send()
                beside(chunk, gene).wait_send()

            @pl.when(z + distance < line)
            def _():
                gene = me + 4 * distance
                pl.when(z > 0)(lambda: down(chunk, gene).wait_send())
                across(chunk, gene).wait_send()
                beside(chunk, gene).wait_send()

        for at in range(line):
            beside(chunk, at * 4 + other_x).wait_send()


def exchange(shard, table, which):
    groups, cells = lax.axis_size("genes"), lax.axis_size("cells")
    per_dev, cell_rows, width = shard.shape
    entries = table.shape[0] // cells
    if groups % 4 or groups < 8 or cell_rows % 8:
        whole = lax.all_gather(shard, "genes", axis=0, tiled=True)
        picked = jnp.take(whole, table, axis=0)
        return lax.all_to_all(picked, "cells", split_axis=0, concat_axis=1, tiled=True)
    chunks = max(c for c in range(1, 6) if cell_rows % (8 * c) == 0)
    size = cell_rows // chunks
    dma = pltpu.SemaphoreType.DMA
    return pl.pallas_call(
        functools.partial(exchange_kernel, chunks),
        out_shape=jax.ShapeDtypeStruct((entries, cells * cell_rows, width), shard.dtype),
        in_specs=[
            pl.BlockSpec(memory_space=pltpu.SMEM),
            pl.BlockSpec(memory_space=pltpu.VMEM),
        ],
        out_specs=pl.BlockSpec(memory_space=pltpu.VMEM),
        scratch_shapes=[pltpu.VMEM((groups * per_dev, size, width), shard.dtype)] * chunks
        + [pltpu.VMEM((cells - 1, entries, size, width), shard.dtype)] * chunks
        + [
            dma((chunks, groups, 2)),
            dma((chunks, groups)),
            dma((chunks, groups)),
            dma((chunks, groups)),
            dma((chunks, cells)),
            dma((chunks, cells)),
            dma((chunks,)),
        ],
        compiler_params=pltpu.CompilerParams(
            collective_id=which, has_side_effects=True, vmem_limit_bytes=60 << 20
        ),
    )(table, shard)


def per_device(expression, omega_diag, omega_offd, omega_src, omega_off):
    high = lax.Precision.HIGH
    here = lax.axis_index("genes")
    where = lax.axis_index("cells")
    cells = lax.axis_size("cells")
    per_dev, width = omega_diag.shape[:2]
    fan = omega_src.shape[1]
    cell_rows = expression.shape[0]
    share = per_dev // cells
    all_rows = cells * cell_rows
    rows = stored_rows(omega_src, omega_off, per_dev)
    table = lax.dynamic_slice_in_dim(rows, here * per_dev, per_dev, 0).reshape(-1)
    mine_diag = lax.dynamic_slice_in_dim(omega_diag, where * share, share, 0)
    mine_off = lax.dynamic_slice_in_dim(omega_offd, where * share, share, 0)

    shard_x = jnp.swapaxes(expression.reshape(cell_rows, per_dev, width), 0, 1)
    own_x = lax.all_to_all(shard_x, "cells", split_axis=0, concat_axis=1, tiled=True)
    far_x = exchange(shard_x, table, 0).reshape(share, fan, all_rows, width)
    own_y = jnp.einsum("jcb,jbe->jce", own_x, mine_diag, precision=high)
    own_y = own_y + jnp.einsum("jkcb,jkbe->jce", far_x, mine_off, precision=high)
    shard_y = lax.all_to_all(own_y, "cells", split_axis=1, concat_axis=0, tiled=True)
    far_y = exchange(shard_y, table, 1).reshape(share, fan, all_rows, width)
    diag_sum = jnp.einsum("jcb,jce->jbe", own_x, own_y, precision=high)
    diag_sum = diag_sum + jnp.swapaxes(diag_sum, 1, 2)
    off_sum = jnp.einsum("jkcb,jce->jkbe", far_x, own_y, precision=high)
    off_sum = off_sum + jnp.einsum("jkcb,jce->jkbe", far_y, own_x, precision=high)

    step_size = 0.5
    limit = step_size * 0.04
    scale = 1.0 / (2.0 * all_rows)
    eye = (
        lax.broadcasted_iota(jnp.int32, (width, width), 0)
        == lax.broadcasted_iota(jnp.int32, (width, width), 1)
    ).astype(jnp.float32)
    entries = jnp.sum(mine_diag * eye, axis=2)
    grad_diag = diag_sum * scale - eye * (1.0 / entries)[:, :, None]
    moved = mine_diag - step_size * grad_diag
    new_diag = eye * moved + (1.0 - eye) * shrink(moved, limit)
    new_offd = shrink(mine_off - step_size * (off_sum * scale), limit)
    return (new_diag, new_offd)


def solution(mesh):
    return jax.shard_map(
        per_device,
        mesh=mesh,
        in_specs=(
            P("cells", "genes"),
            P("genes", None, None),
            P("genes", None, None, None),
            P(),
            P(),
        ),
        out_specs=(P(("genes", "cells"), None, None), P(("genes", "cells"), None, None, None)),
        check_vma=False,
    )
```

```python
import functools

import jax
import jax.numpy as jnp
from jax import lax
from jax.experimental import pallas as pl
from jax.experimental.pallas import tpu as pltpu
from jax.sharding import PartitionSpec as P

MESH = pl.DeviceIdType.MESH


def stored_rows(omega_src, omega_off, per_dev):
    cols = lax.broadcasted_iota(jnp.int32, omega_src.shape, 0)
    bump = jnp.logical_and(omega_src == cols // per_dev, omega_off >= cols % per_dev).astype(
        jnp.int32
    )
    return omega_src * per_dev + omega_off + bump


def shrink(values, limit):
    return values - jnp.clip(values, -limit, limit)


def exchange_kernel(chunks, table_ref, shard_ref, far_ref, *scratch):
    held, picked = scratch[:chunks], scratch[chunks : 2 * chunks]
    z_send, x_send, k_send, got, c_send, c_got, own_sem = scratch[2 * chunks :]
    groups, cells = lax.axis_size("genes"), lax.axis_size("cells")
    me, part = lax.axis_index("genes"), lax.axis_index("cells")
    line = groups // 4
    per_dev, cell_rows, _ = shard_ref.shape
    size = cell_rows // chunks
    entries = far_ref.shape[0]
    z, lane = me // 4, me % 4
    other_x = lane + 2 - 4 * (lane // 2)
    other_k = me + 1 - 2 * (me % 2)
    x_peer = z * 4 + other_x

    def to_gene(gene):
        return (part, gene)

    def to_cell(step):
        return ((part + step) % cells, me)

    barrier = pltpu.get_barrier_semaphore()
    ahead, behind = (z + 1) % line * 4 + lane, (z + line - 1) % line * 4 + lane
    for gene in (ahead, behind, x_peer, other_k):
        pl.semaphore_signal(barrier, inc=1, device_id=to_gene(gene), device_id_type=MESH)
    for step in range(1, cells):
        pl.semaphore_signal(barrier, inc=1, device_id=to_cell(step), device_id_type=MESH)
    pl.semaphore_wait(barrier, 4 + cells - 1)

    def seat(chunk, gene):
        return held[chunk].at[pl.ds(gene * per_dev, per_dev)]

    def own(chunk):
        return shard_ref.at[:, pl.ds(chunk * size, size), :]

    def copy(chunk, gene, send_sem, target, first=False):
        return pltpu.make_async_remote_copy(
            src_ref=own(chunk) if first else seat(chunk, gene),
            dst_ref=seat(chunk, gene),
            send_sem=send_sem,
            recv_sem=got.at[chunk, gene],
            device_id=to_gene(target),
            device_id_type=MESH,
        )

    def arrive(chunk, gene):
        copy(chunk, gene, k_send.at[chunk, gene], other_k).wait_recv()

    def keep(chunk):
        return pltpu.make_async_copy(own(chunk), seat(chunk, me), own_sem.at[chunk])

    def up(chunk, gene, first=False):
        return copy(chunk, gene, z_send.at[chunk, gene, 0], me + 4, first)

    def down(chunk, gene, first=False):
        return copy(chunk, gene, z_send.at[chunk, gene, 1], me - 4, first)

    def across(chunk, gene, first=False):
        return copy(chunk, gene, x_send.at[chunk, gene], x_peer, first)

    def beside(chunk, gene, first=False):
        return copy(chunk, gene, k_send.at[chunk, gene], other_k, first)

    def start_own(chunk):
        pl.when(z < line - 1)(lambda: up(chunk, me, True).start())
        pl.when(z > 0)(lambda: down(chunk, me, True).start())
        across(chunk, me, True).start()
        beside(chunk, me, True).start()
        keep(chunk).start()

    def turned(chunk):
        return chunk % 5 == 3

    def lanes(chunk):
        return (0, other_x - lane) if turned(chunk) else (0,)

    def line_hops(chunk, distance, act):
        def hops(gene, edge, onward):
            for shift in lanes(chunk):
                act[0](chunk, gene + shift)
                pl.when(edge)(lambda: act[1](onward(chunk, gene + shift)))
                if not turned(chunk):
                    act[1](across(chunk, gene))
                act[1](beside(chunk, gene + shift))

        pl.when(z - distance >= 0)(lambda: hops(me - 4 * distance, z < line - 1, up))
        pl.when(z + distance < line)(lambda: hops(me + 4 * distance, z > 0, down))

    def cross_hops(chunk, act):
        for at in range(1 if turned(chunk) else line):
            gene = x_peer if turned(chunk) else at * 4 + other_x
            act[0](chunk, gene)
            if turned(chunk):
                pl.when(z < line - 1)(lambda: act[1](up(chunk, gene)))
                pl.when(z > 0)(lambda: act[1](down(chunk, gene)))
            act[1](beside(chunk, gene))

    start = (arrive, lambda c: c.start())
    finish = (lambda chunk, gene: None, lambda c: c.wait_send())

    def row_span(chunk, cell):
        return pl.ds(pl.multiple_of(cell * cell_rows + chunk * size, 8), size)

    def hand(chunk, step):
        return pltpu.make_async_remote_copy(
            src_ref=picked[chunk].at[step - 1],
            dst_ref=far_ref.at[:, row_span(chunk, part), :],
            send_sem=c_send.at[chunk, step],
            recv_sem=c_got.at[chunk, step],
            device_id=to_cell(step),
            device_id_type=MESH,
        )

    def pick(chunk):
        keep(chunk).wait()
        for at in range(line):
            for side in range(2):
                arrive(chunk, at * 4 + side * 2 + other_k % 2)
        for step in list(range(1, cells)) + [0]:
            base = (part + step) % cells * entries

            def body(entry, carry):
                block = held[chunk][table_ref[base + entry]]
                if step == 0:
                    far_ref[entry, row_span(chunk, part), :] = block
                else:
                    picked[chunk][step - 1, entry] = block
                return carry

            lax.fori_loop(0, entries, body, 0)
            if step:
                hand(chunk, step).start()

    for t in range(chunks + line + 1):
        if t < chunks:
            start_own(t)
        if t >= 1 and t - 1 < chunks and turned(t - 1):
            cross_hops(t - 1, start)
        for distance in range(1, line):
            chunk = t - distance
            if 0 <= chunk < chunks:
                line_hops(chunk, distance, start)
        if 0 <= t - line < chunks and not turned(t - line):
            cross_hops(t - line, start)
        if 0 <= t - line - 1 < chunks:
            pick(t - line - 1)

    for chunk in range(chunks):
        for step in range(1, cells):
            hand(chunk, step).wait_recv()
            hand(chunk, step).wait_send()
        pl.when(z < line - 1)(lambda: up(chunk, me, True).wait_send())
        pl.when(z > 0)(lambda: down(chunk, me, True).wait_send())
        across(chunk, me, True).wait_send()
        beside(chunk, me, True).wait_send()
        for distance in range(1, line):
            line_hops(chunk, distance, finish)
        cross_hops(chunk, finish)


def exchange(shard, table, which):
    groups, cells = lax.axis_size("genes"), lax.axis_size("cells")
    per_dev, cell_rows, width = shard.shape
    entries = table.shape[0] // cells
    if groups % 4 or groups < 8 or cell_rows % 8:
        whole = lax.all_gather(shard, "genes", axis=0, tiled=True)
        picked = jnp.take(whole, table, axis=0)
        return lax.all_to_all(picked, "cells", split_axis=0, concat_axis=1, tiled=True)
    chunks = max(c for c in range(1, 11) if cell_rows % (8 * c) == 0)
    size = cell_rows // chunks
    dma = pltpu.SemaphoreType.DMA
    return pl.pallas_call(
        functools.partial(exchange_kernel, chunks),
        out_shape=jax.ShapeDtypeStruct((entries, cells * cell_rows, width), shard.dtype),
        in_specs=[
            pl.BlockSpec(memory_space=pltpu.SMEM),
            pl.BlockSpec(memory_space=pltpu.VMEM),
        ],
        out_specs=pl.BlockSpec(memory_space=pltpu.VMEM),
        scratch_shapes=[pltpu.VMEM((groups * per_dev, size, width), shard.dtype)] * chunks
        + [pltpu.VMEM((cells - 1, entries, size, width), shard.dtype)] * chunks
        + [
            dma((chunks, groups, 2)),
            dma((chunks, groups)),
            dma((chunks, groups)),
            dma((chunks, groups)),
            dma((chunks, cells)),
            dma((chunks, cells)),
            dma((chunks,)),
        ],
        compiler_params=pltpu.CompilerParams(
            collective_id=which, has_side_effects=True, vmem_limit_bytes=60 << 20
        ),
    )(table, shard)


def per_device(expression, omega_diag, omega_offd, omega_src, omega_off):
    high = lax.Precision.HIGH
    here = lax.axis_index("genes")
    where = lax.axis_index("cells")
    cells = lax.axis_size("cells")
    per_dev, width = omega_diag.shape[:2]
    fan = omega_src.shape[1]
    cell_rows = expression.shape[0]
    share = per_dev // cells
    all_rows = cells * cell_rows
    rows = stored_rows(omega_src, omega_off, per_dev)
    table = lax.dynamic_slice_in_dim(rows, here * per_dev, per_dev, 0).reshape(-1)
    mine_diag = lax.dynamic_slice_in_dim(omega_diag, where * share, share, 0)
    mine_off = lax.dynamic_slice_in_dim(omega_offd, where * share, share, 0)

    shard_x = jnp.swapaxes(expression.reshape(cell_rows, per_dev, width), 0, 1)
    own_x = lax.all_to_all(shard_x, "cells", split_axis=0, concat_axis=1, tiled=True)
    far_x = exchange(shard_x, table, 0).reshape(share, fan, all_rows, width)
    own_y = jnp.einsum("jcb,jbe->jce", own_x, mine_diag, precision=high)
    own_y = own_y + jnp.einsum("jkcb,jkbe->jce", far_x, mine_off, precision=high)
    shard_y = lax.all_to_all(own_y, "cells", split_axis=1, concat_axis=0, tiled=True)
    far_y = exchange(shard_y, table, 1).reshape(share, fan, all_rows, width)
    diag_sum = jnp.einsum("jcb,jce->jbe", own_x, own_y, precision=high)
    diag_sum = diag_sum + jnp.swapaxes(diag_sum, 1, 2)
    off_sum = jnp.einsum("jkcb,jce->jkbe", far_x, own_y, precision=high)
    off_sum = off_sum + jnp.einsum("jkcb,jce->jkbe", far_y, own_x, precision=high)

    step_size = 0.5
    limit = step_size * 0.04
    scale = 1.0 / (2.0 * all_rows)
    eye = (
        lax.broadcasted_iota(jnp.int32, (width, width), 0)
        == lax.broadcasted_iota(jnp.int32, (width, width), 1)
    ).astype(jnp.float32)
    entries = jnp.sum(mine_diag * eye, axis=2)
    grad_diag = diag_sum * scale - eye * (1.0 / entries)[:, :, None]
    moved = mine_diag - step_size * grad_diag
    new_diag = eye * moved + (1.0 - eye) * shrink(moved, limit)
    new_offd = shrink(mine_off - step_size * (off_sum * scale), limit)
    return (new_diag, new_offd)


def solution(mesh):
    return jax.shard_map(
        per_device,
        mesh=mesh,
        in_specs=(
            P("cells", "genes"),
            P("genes", None, None),
            P("genes", None, None, None),
            P(),
            P(),
        ),
        out_specs=(P(("genes", "cells"), None, None), P(("genes", "cells"), None, None, None)),
        check_vma=False,
    )
```

```python
import functools

import jax
import jax.numpy as jnp
from jax import lax
from jax.experimental import pallas as pl
from jax.experimental.pallas import tpu as pltpu
from jax.sharding import PartitionSpec as P

MESH = pl.DeviceIdType.MESH


def stored_rows(omega_src, omega_off, per_dev):
    cols = lax.broadcasted_iota(jnp.int32, omega_src.shape, 0)
    bump = jnp.logical_and(omega_src == cols // per_dev, omega_off >= cols % per_dev).astype(
        jnp.int32
    )
    return omega_src * per_dev + omega_off + bump


def shrink(values, limit):
    return values - jnp.clip(values, -limit, limit)


def exchange_kernel(chunks, table_ref, shard_ref, far_ref, *scratch):
    held, picked = scratch[:chunks], scratch[chunks : 2 * chunks]
    z_send, x_send, k_send, got, c_send, c_got, own_sem = scratch[2 * chunks :]
    groups, cells = lax.axis_size("genes"), lax.axis_size("cells")
    me, part = lax.axis_index("genes"), lax.axis_index("cells")
    line = groups // 4
    per_dev, cell_rows, _ = shard_ref.shape
    size = cell_rows // chunks
    entries = far_ref.shape[0]
    z, lane = me // 4, me % 4
    other_x = lane + 2 - 4 * (lane // 2)
    other_k = me + 1 - 2 * (me % 2)
    x_peer = z * 4 + other_x

    def to_gene(gene):
        return (part, gene)

    def to_cell(step):
        return ((part + step) % cells, me)

    barrier = pltpu.get_barrier_semaphore()
    ahead, behind = (z + 1) % line * 4 + lane, (z + line - 1) % line * 4 + lane
    for gene in (ahead, behind, x_peer, other_k):
        pl.semaphore_signal(barrier, inc=1, device_id=to_gene(gene), device_id_type=MESH)
    for step in range(1, cells):
        pl.semaphore_signal(barrier, inc=1, device_id=to_cell(step), device_id_type=MESH)
    pl.semaphore_wait(barrier, 4 + cells - 1)

    def seat(chunk, gene):
        return held[chunk].at[pl.ds(gene * per_dev, per_dev)]

    def own(chunk):
        return shard_ref.at[:, pl.ds(chunk * size, size), :]

    def copy(chunk, gene, send_sem, target, first=False):
        return pltpu.make_async_remote_copy(
            src_ref=own(chunk) if first else seat(chunk, gene),
            dst_ref=seat(chunk, gene),
            send_sem=send_sem,
            recv_sem=got.at[chunk, gene],
            device_id=to_gene(target),
            device_id_type=MESH,
        )

    def arrive(chunk, gene):
        copy(chunk, gene, k_send.at[chunk, gene], other_k).wait_recv()

    def keep(chunk):
        return pltpu.make_async_copy(own(chunk), seat(chunk, me), own_sem.at[chunk])

    def up(chunk, gene, first=False):
        return copy(chunk, gene, z_send.at[chunk, gene, 0], me + 4, first)

    def down(chunk, gene, first=False):
        return copy(chunk, gene, z_send.at[chunk, gene, 1], me - 4, first)

    def across(chunk, gene, first=False):
        return copy(chunk, gene, x_send.at[chunk, gene], x_peer, first)

    def beside(chunk, gene, first=False):
        return copy(chunk, gene, k_send.at[chunk, gene], other_k, first)

    def start_own(chunk):
        pl.when(z < line - 1)(lambda: up(chunk, me, True).start())
        pl.when(z > 0)(lambda: down(chunk, me, True).start())
        across(chunk, me, True).start()
        beside(chunk, me, True).start()
        keep(chunk).start()

    def turned(chunk):
        return chunk % 5 == 3

    def lanes(chunk):
        return (0, other_x - lane) if turned(chunk) else (0,)

    def line_hops(chunk, distance, act):
        def hops(gene, edge, onward):
            for shift in lanes(chunk):
                act[0](chunk, gene + shift)
                pl.when(edge)(lambda: act[1](onward(chunk, gene + shift)))
                if not turned(chunk):
                    act[1](across(chunk, gene))
                act[1](beside(chunk, gene + shift))

        pl.when(z - distance >= 0)(lambda: hops(me - 4 * distance, z < line - 1, up))
        pl.when(z + distance < line)(lambda: hops(me + 4 * distance, z > 0, down))

    def cross_hops(chunk, act):
        for at in range(1 if turned(chunk) else line):
            gene = x_peer if turned(chunk) else at * 4 + other_x
            act[0](chunk, gene)
            if turned(chunk):
                pl.when(z < line - 1)(lambda: act[1](up(chunk, gene)))
                pl.when(z > 0)(lambda: act[1](down(chunk, gene)))
            act[1](beside(chunk, gene))

    start = (arrive, lambda c: c.start())
    finish = (lambda chunk, gene: None, lambda c: c.wait_send())

    def row_span(chunk, cell):
        return pl.ds(pl.multiple_of(cell * cell_rows + chunk * size, 8), size)

    def hand(chunk, step):
        return pltpu.make_async_remote_copy(
            src_ref=picked[chunk].at[step - 1],
            dst_ref=far_ref.at[:, row_span(chunk, part), :],
            send_sem=c_send.at[chunk, step],
            recv_sem=c_got.at[chunk, step],
            device_id=to_cell(step),
            device_id_type=MESH,
        )

    def pick(chunk):
        keep(chunk).wait()
        for at in range(line):
            for side in range(2):
                arrive(chunk, at * 4 + side * 2 + other_k % 2)
        for step in list(range(1, cells)) + [0]:
            base = (part + step) % cells * entries

            def body(entry, carry):
                block = held[chunk][table_ref[base + entry]]
                if step == 0:
                    far_ref[entry, row_span(chunk, part), :] = block
                else:
                    picked[chunk][step - 1, entry] = block
                return carry

            lax.fori_loop(0, entries, body, 0)
            if step:
                hand(chunk, step).start()

    for t in range(chunks + line):
        if t < chunks:
            start_own(t)
        if t >= 1 and t - 1 < chunks and turned(t - 1):
            cross_hops(t - 1, start)
        for distance in range(1, line):
            chunk = t - distance
            if 0 <= chunk < chunks:
                line_hops(chunk, distance, start)
        if 0 <= t - line < chunks and not turned(t - line):
            cross_hops(t - line, start)
        if 0 <= t - line < chunks:
            pick(t - line)

    for chunk in range(chunks):
        for step in range(1, cells):
            hand(chunk, step).wait_recv()
            hand(chunk, step).wait_send()
        pl.when(z < line - 1)(lambda: up(chunk, me, True).wait_send())
        pl.when(z > 0)(lambda: down(chunk, me, True).wait_send())
        across(chunk, me, True).wait_send()
        beside(chunk, me, True).wait_send()
        for distance in range(1, line):
            line_hops(chunk, distance, finish)
        cross_hops(chunk, finish)


def exchange(shard, table, which):
    groups, cells = lax.axis_size("genes"), lax.axis_size("cells")
    per_dev, cell_rows, width = shard.shape
    entries = table.shape[0] // cells
    if groups % 4 or groups < 8 or cell_rows % 8:
        whole = lax.all_gather(shard, "genes", axis=0, tiled=True)
        picked = jnp.take(whole, table, axis=0)
        return lax.all_to_all(picked, "cells", split_axis=0, concat_axis=1, tiled=True)
    chunks = max(c for c in range(1, 11) if cell_rows % (8 * c) == 0)
    size = cell_rows // chunks
    dma = pltpu.SemaphoreType.DMA
    return pl.pallas_call(
        functools.partial(exchange_kernel, chunks),
        out_shape=jax.ShapeDtypeStruct((entries, cells * cell_rows, width), shard.dtype),
        in_specs=[
            pl.BlockSpec(memory_space=pltpu.SMEM),
            pl.BlockSpec(memory_space=pltpu.VMEM),
        ],
        out_specs=pl.BlockSpec(memory_space=pltpu.VMEM),
        scratch_shapes=[pltpu.VMEM((groups * per_dev, size, width), shard.dtype)] * chunks
        + [pltpu.VMEM((cells - 1, entries, size, width), shard.dtype)] * chunks
        + [
            dma((chunks, groups, 2)),
            dma((chunks, groups)),
            dma((chunks, groups)),
            dma((chunks, groups)),
            dma((chunks, cells)),
            dma((chunks, cells)),
            dma((chunks,)),
        ],
        compiler_params=pltpu.CompilerParams(
            collective_id=which, has_side_effects=True, vmem_limit_bytes=60 << 20
        ),
    )(table, shard)


def per_device(expression, omega_diag, omega_offd, omega_src, omega_off):
    high = lax.Precision.HIGH
    here = lax.axis_index("genes")
    where = lax.axis_index("cells")
    cells = lax.axis_size("cells")
    per_dev, width = omega_diag.shape[:2]
    fan = omega_src.shape[1]
    cell_rows = expression.shape[0]
    share = per_dev // cells
    all_rows = cells * cell_rows
    rows = stored_rows(omega_src, omega_off, per_dev)
    table = lax.dynamic_slice_in_dim(rows, here * per_dev, per_dev, 0).reshape(-1)
    mine_diag = lax.dynamic_slice_in_dim(omega_diag, where * share, share, 0)
    mine_off = lax.dynamic_slice_in_dim(omega_offd, where * share, share, 0)

    shard_x = jnp.swapaxes(expression.reshape(cell_rows, per_dev, width), 0, 1)
    own_x = lax.all_to_all(shard_x, "cells", split_axis=0, concat_axis=1, tiled=True)
    far_x = exchange(shard_x, table, 0).reshape(share, fan, all_rows, width)
    own_y = jnp.einsum("jcb,jbe->jce", own_x, mine_diag, precision=high)
    own_y = own_y + jnp.einsum("jkcb,jkbe->jce", far_x, mine_off, precision=high)
    shard_y = lax.all_to_all(own_y, "cells", split_axis=1, concat_axis=0, tiled=True)
    far_y = exchange(shard_y, table, 1).reshape(share, fan, all_rows, width)
    diag_sum = jnp.einsum("jcb,jce->jbe", own_x, own_y, precision=high)
    diag_sum = diag_sum + jnp.swapaxes(diag_sum, 1, 2)
    off_sum = jnp.einsum("jkcb,jce->jkbe", far_x, own_y, precision=high)
    off_sum = off_sum + jnp.einsum("jkcb,jce->jkbe", far_y, own_x, precision=high)

    step_size = 0.5
    limit = step_size * 0.04
    scale = 1.0 / (2.0 * all_rows)
    eye = (
        lax.broadcasted_iota(jnp.int32, (width, width), 0)
        == lax.broadcasted_iota(jnp.int32, (width, width), 1)
    ).astype(jnp.float32)
    entries = jnp.sum(mine_diag * eye, axis=2)
    grad_diag = diag_sum * scale - eye * (1.0 / entries)[:, :, None]
    moved = mine_diag - step_size * grad_diag
    new_diag = eye * moved + (1.0 - eye) * shrink(moved, limit)
    new_offd = shrink(mine_off - step_size * (off_sum * scale), limit)
    return (new_diag, new_offd)


def solution(mesh):
    return jax.shard_map(
        per_device,
        mesh=mesh,
        in_specs=(
            P("cells", "genes"),
            P("genes", None, None),
            P("genes", None, None, None),
            P(),
            P(),
        ),
        out_specs=(P(("genes", "cells"), None, None), P(("genes", "cells"), None, None, None)),
        check_vma=False,
    )
```
